256 devices in a mesh: gz: 32 (over z, y), ex: 8 (over x, core).
Axes of the slice: x: 4, y: 4, z: 8, core: 2. Of those that a mesh axis runs over, the one named last changes fastest.
Arguments:
- tokens: bfloat16 [256, 128, 1152], P('ex', 'gz'), may hold values from -12 to 12
- modulation: float32 [6, 1152], replicated, may hold values from -3 to 3
- w_qkv: bfloat16 [3, 1152, 1152], P(None, None, 'ex'), may hold values from -0.1875 to 0.1875
- w_proj: bfloat16 [1152, 1152], P('ex'), may hold values from -0.1875 to 0.1875
- phase: int32 [16], replicated, may hold values from 0 to 3
- routes: int32 [8, 32, 128, 2], P('ex', 'gz'), may hold values from 0 to 7, all different within a row; in each aligned block of 128 rows (0 to 127, 128 to 255, ..., all dimensions but the last counted through in order) at most 64 rows name the same one
- gates: float32 [8, 32, 128, 2], P('ex', 'gz'), may hold values from 0.2 to 1
- w_in: bfloat16 [8, 4608, 1152], P('ex', 'gz'), may hold values from -0.1875 to 0.1875
- w_out: bfloat16 [8, 4608, 1152], P('ex', 'gz'), may hold values from -0.09375 to 0.09375
Outputs:
- updated: bfloat16 [256, 128, 1152], P('ex', 'gz')
The draws below stay inside these ranges and needn't reach their ends.
Inputs may be any that keep to these rules, and one draw needn't show every extreme that they name: Among the rows of one device no expert is named by more than 64 routes, and in every draw some expert is named by exactly 64 routes of one device.
All inputs are finite; a program needn't handle non-finite values.
Results may differ from the reference program's by a relative error of at most 0.0049.
Values may be sent and summed in bfloat16 or wider, within the bound.
A program may use at most 128 MiB of HBM per device.

```python
import math
import jax
import jax.numpy as jnp
import numpy as np
from jax import lax

D = 1152
HEADS = 16
FF = 4608
HEAD_DIM = 72
TOP = 2
TILE = 16
WZ = 4
SZ = 4
XY_DEV = 32
TOK_DEV = 128
COLS = 256
TILES_ALL = 16
NZ = 128
EXPERTS = 8
CAP = 64
N_GZ = 32
N_EX = 8


def draw_tokens(key, part):
    keys = jax.random.split(key, 3)
    low = math.log(0.3)
    high = math.log(3.0)
    column_scale = jnp.exp(jax.random.uniform(keys[0], (1, 1, D), jnp.float32, low, high))
    row_scale = jnp.exp(jax.random.uniform(keys[1], (COLS, NZ, 1), jnp.float32, low, high))
    values = jax.random.normal(keys[2], (COLS, NZ, D), jnp.float32) * column_scale * row_scale
    return jnp.clip(values, -12.0, 12.0).astype(jnp.bfloat16)


def place_ends(values, rng, least, largest):
    longest = values.shape.index(max(values.shape))
    spots = []
    for shift in (0, 1):
        where = [jax.random.randint(jax.random.fold_in(rng, axis), (), 0, length) for axis, length in enumerate(values.shape)]
        where[longest] = (where[longest] + shift) % values.shape[longest]
        spots.append(tuple(where))
    return values.at[spots[0]].set(least).at[spots[1]].set(largest)


def level_of(key, shape, shards, low, high):
    def one(position, shards_of):
        heights = jax.random.uniform(jax.random.fold_in(jax.random.fold_in(key, 6), position), (shards_of,), jnp.float32, low / len(shards), high / len(shards))
        return jnp.repeat(jnp.exp(heights), shape[position] // shards_of).reshape((-1,) + (1,) * (len(shape) - position - 1))

    level = one(*shards[0])
    for cut in shards[1:]:
        level = level * one(*cut)
    return level


def shared_out(rng, own, number, rows, number_of, top, reach, skew):
    order = jax.random.permutation(rng, number_of)
    packed, usual = portions_of(number_of, rows * top, reach, skew, True), portions_of(number_of, rows * top, reach, skew, False)
    places = jnp.arange(number_of)

    def named(lengths, turn):
        used = int((lengths > 0).sum())
        fixed = max(1, used // 4)
        passed = fixed + (places - fixed + turn * (used - fixed)) % max(1, number_of - fixed)
        return jnp.zeros((number_of,), jnp.int32).at[order[jnp.where(places < fixed, places, passed)]].set(jnp.asarray(lengths, jnp.int32))

    lengths = jnp.where(number % 4 == 0, named(packed, number // 4), named(usual, number - number // 4 - 1))
    mixed = jax.random.permutation(jax.random.fold_in(own, 3), number_of)
    giver, receiver = mixed[0:number_of // 2 * 2:2], mixed[1:number_of // 2 * 2:2]
    margin = jnp.minimum(lengths[giver] - 1, reach - lengths[receiver]) // 2
    margin = jnp.where((giver == order[0]) | (receiver == order[0]) | (lengths[receiver] == 0), 0, jnp.maximum(margin, 0))
    passed = jax.random.randint(jax.random.fold_in(own, 4), (number_of // 2,), 0, 1 << 20) % (margin + 1)
    lengths = lengths.at[giver].add(-passed).at[receiver].add(passed)
    members = jnp.searchsorted(jnp.cumsum(lengths), jnp.arange(rows * top), side="right").astype(jnp.int32)
    grid = members.reshape(top, rows).T
    grid = grid[jax.random.permutation(jax.random.fold_in(own, 1), rows)]
    turn = jax.random.randint(jax.random.fold_in(own, 2), (rows, 1), 0, top)
    return jnp.take_along_axis(grid, (jnp.arange(top)[None, :] + turn) % top, axis=1)


def portions_of(amount, total, reach, slope, full):
    portions = [(1 << 20) // math.isqrt(standing ** slope) + 1 for standing in range(1, amount + 1)]
    largest = reach if full else min(reach, max(-(-total // amount), total * portions[0] // sum(portions)))
    least = 1 if total - largest >= amount - 1 else 0
    holding, surplus = [largest] + [least] * (amount - 1), total - largest - least * (amount - 1)
    while surplus > 0:
        candidates = [i for i in range(1, amount) if holding[i] < largest] or [i for i in range(1, amount) if holding[i] < reach]
        pool, budget = sum([portions[i] for i in candidates]), surplus
        for i in candidates:
            extra = min(reach - holding[i], max(1, budget * portions[i] // pool), surplus)
            holding[i] = holding[i] + extra
            surplus = surplus - extra
    return np.array(holding)


def normal_values(stream_key, dims, scale, bound, shards=(), held_as=jnp.bfloat16):
    level = level_of(stream_key, dims, shards, -0.22, 0.18) if shards else 1.0
    drawn = jax.random.normal(stream_key, dims, jnp.float32) * scale * level
    return jnp.minimum(jnp.maximum(drawn, -bound), bound).astype(held_as)


def setup_inputs(seed: int = 0) -> dict:
    splits = jax.random.split(jax.random.key(seed), 10)
    tokens = draw_tokens(jax.random.fold_in(splits[9], 71), 0)
    modulation = normal_values(splits[1], (6, D), 0.5, 3.0, (), jnp.float32)
    w_qkv = normal_values(splits[2], (3, D, D), D ** -0.5, 0.1875, ((2, 8),))
    w_proj = normal_values(splits[3], (D, D), D ** -0.5, 0.1875, ((0, 8),))
    phase = place_ends(jax.random.randint(splits[4], (TILES_ALL,), 0, WZ), jax.random.fold_in(splits[4], 1), 0, WZ - 1).astype(jnp.int32)
    routes_keys = jax.random.split(jax.random.fold_in(splits[5], 1), N_EX * N_GZ * TOK_DEV // TOK_DEV)
    routes_turns = jax.random.permutation(jax.random.fold_in(splits[5], 3), N_EX * N_GZ * TOK_DEV // TOK_DEV)
    routes = jax.vmap(lambda own, number: shared_out(jax.random.fold_in(splits[5], 2), own, number, TOK_DEV, EXPERTS, TOP, CAP, 2))(routes_keys, routes_turns).reshape((N_EX, N_GZ, TOK_DEV, TOP))
    gates = jnp.clip(0.2 + 0.8 * jax.random.uniform(splits[6], (N_EX, N_GZ, TOK_DEV, TOP), jnp.float32) ** level_of(splits[6], (N_EX, N_GZ, TOK_DEV, TOP), ((0, 8), (1, 32)), -0.2, 0.2), 0.2, 1.0)
    w_in = normal_values(splits[7], (EXPERTS, FF, D), D ** -0.5, 0.1875, ((0, 8), (1, 32)))
    w_out = normal_values(splits[8], (EXPERTS, FF, D), FF ** -0.5, 0.09375, ((0, 8), (1, 32)))
    return dict(tokens=tokens, modulation=modulation, w_qkv=w_qkv, w_proj=w_proj, phase=phase, routes=routes, gates=gates, w_in=w_in, w_out=w_out)


EPS = 1e-06

def layer_norm(values):
    center = lax.optimization_barrier(jnp.mean(values, axis=-1, keepdims=True))
    centered = values - center
    spread = lax.optimization_barrier(jnp.mean(centered * centered, axis=-1, keepdims=True))
    return centered / jnp.sqrt(spread + EPS)

def head_norm(values):
    return values / jnp.sqrt(lax.optimization_barrier(jnp.mean(values * values, axis=-1, keepdims=True)) + EPS)

def modulate(values, shift, scale):
    return layer_norm(values) * (1.0 + scale) + shift

def tile_mix(tile_tokens, tile_phase, w_qkv, w_proj, modulation):
    normed = modulate(tile_tokens.astype(jnp.float32), modulation[0], modulation[1]).astype(jnp.bfloat16)
    flattened = normed.reshape(TILE * NZ, D)
    queries = jnp.dot(flattened, w_qkv[0], preferred_element_type=jnp.float32).reshape(TILE, NZ, HEADS, HEAD_DIM)
    key_part = jnp.dot(flattened, w_qkv[1], preferred_element_type=jnp.float32).reshape(TILE, NZ, HEADS, HEAD_DIM)
    value_part = jnp.dot(flattened, w_qkv[2], preferred_element_type=jnp.float32).reshape(TILE, NZ, HEADS, HEAD_DIM)
    queries = head_norm(queries).astype(jnp.bfloat16)
    key_part = head_norm(key_part).astype(jnp.bfloat16)
    value_part = value_part.astype(jnp.bfloat16)
    padded_depth = NZ + WZ
    window_count = padded_depth // WZ
    anchor = jnp.zeros((), jnp.int32)
    first_plane = tile_phase.astype(jnp.int32)

    def settle(array):
        canvas = jnp.zeros((TILE, padded_depth, HEADS, HEAD_DIM), array.dtype)
        placed = lax.dynamic_update_slice(canvas, array, (anchor, first_plane, anchor, anchor))
        grouped = placed.reshape(TILE, window_count, WZ, HEADS, HEAD_DIM).transpose(1, 2, 0, 3, 4)
        return grouped.reshape(window_count, WZ * TILE, HEADS, HEAD_DIM)
    query_win = settle(queries)
    key_win = settle(key_part)
    value_win = settle(value_part)
    planes_all = jnp.arange(padded_depth, dtype=jnp.int32)
    inside = (planes_all >= first_plane) & (planes_all < first_plane + NZ)
    inside = jnp.broadcast_to(inside.reshape(window_count, WZ, 1), (window_count, WZ, TILE)).reshape(window_count, WZ * TILE)
    scores = jnp.einsum('nqhd,nkhd->nhqk', query_win.astype(jnp.float32), key_win.astype(jnp.float32)) * (1.0 / math.sqrt(HEAD_DIM))
    weights_raw = jnp.where(inside[:, None, None, :], jnp.exp(scores), 0.0)
    summed = lax.optimization_barrier(jnp.sum(weights_raw, axis=-1, keepdims=True))
    summed = jnp.where(summed > 0.0, summed, 1.0)
    shares = (weights_raw / summed).astype(jnp.bfloat16)
    mixture = jnp.einsum('nhqk,nkhd->nqhd', shares.astype(jnp.float32), value_win.astype(jnp.float32)).astype(jnp.bfloat16)
    mixture = mixture.reshape(window_count, WZ, TILE, D).reshape(padded_depth, TILE, D)
    mixture = lax.dynamic_slice(mixture, (first_plane, anchor, anchor), (NZ, TILE, D)).transpose(1, 0, 2)
    attended = jnp.dot(mixture.reshape(TILE * NZ, D), w_proj, preferred_element_type=jnp.float32).reshape(TILE, NZ, D)
    return tile_tokens.astype(jnp.float32) + modulation[2] * attended

def reference(tokens, modulation, w_qkv, w_proj, phase, routes, gates, w_in, w_out):
    tiled = tokens.reshape(TILES_ALL, TILE, NZ, D)

    def one_tile(bundle):
        return tile_mix(bundle[0], bundle[1], w_qkv, w_proj, modulation)
    residual = lax.map(one_tile, (tiled, phase)).reshape(COLS, NZ, D)
    block_total = N_EX * N_GZ
    residual_blocks = residual.reshape(N_EX, XY_DEV, N_GZ, SZ, D).transpose(0, 2, 1, 3, 4).reshape(block_total, TOK_DEV, D)
    expert_in = modulate(residual_blocks, modulation[3], modulation[4]).astype(jnp.bfloat16)
    padded_in = jnp.concatenate([expert_in, jnp.zeros((block_total, 1, D), jnp.bfloat16)], axis=1)
    route_ids = routes.reshape(block_total, TOK_DEV, TOP)
    route_gates = gates.reshape(block_total, TOK_DEV, TOP)
    block_rows = jnp.broadcast_to(jnp.arange(block_total, dtype=jnp.int32)[:, None], (block_total, TOK_DEV))
    token_rows = jnp.broadcast_to(jnp.arange(TOK_DEV, dtype=jnp.int32)[None, :], (block_total, TOK_DEV))
    block_slots = jnp.arange(block_total, dtype=jnp.int32)[:, None]

    def expert_pass(running, expert_id):
        hit = route_ids == expert_id
        member = jnp.any(hit, axis=2)
        weight = lax.optimization_barrier(jnp.sum(jnp.where(hit, route_gates, 0.0), axis=2))
        ranking = jnp.cumsum(member.astype(jnp.int32), axis=1) - 1
        spot_index = jnp.where(member, ranking, CAP).astype(jnp.int32)
        slot_table = jnp.full((block_total, CAP), TOK_DEV, jnp.int32).at[block_rows, spot_index].set(token_rows, mode='drop')
        selected = padded_in[block_slots, slot_table]
        hidden = jax.nn.gelu(jnp.dot(selected.reshape(block_total * CAP, D), w_in[expert_id].T, preferred_element_type=jnp.float32), approximate=True).astype(jnp.bfloat16)
        result = jnp.dot(hidden, w_out[expert_id], preferred_element_type=jnp.float32).astype(jnp.bfloat16).reshape(block_total, CAP, D)
        padded_weight = jnp.concatenate([weight, jnp.zeros((block_total, 1), weight.dtype)], axis=1)
        slot_weight = padded_weight[block_slots, slot_table]
        running = running.at[block_slots, slot_table].add(slot_weight[:, :, None] * result.astype(jnp.float32))
        return (running, None)
    moe_sum, _ = lax.scan(expert_pass, jnp.zeros((block_total, TOK_DEV + 1, D), jnp.float32), jnp.arange(EXPERTS, dtype=jnp.int32))
    updated = (residual_blocks + modulation[5] * moe_sum[:, :TOK_DEV]).astype(jnp.bfloat16)
    return updated.reshape(N_EX, N_GZ, XY_DEV, SZ, D).transpose(0, 2, 1, 3, 4).reshape(COLS, NZ, D)
```

```python
import functools
import math

import jax
import jax.numpy as jnp
from jax import lax
from jax.experimental import pallas as pl
from jax.experimental.pallas import tpu as pltpu
from jax.sharding import PartitionSpec as P

D = 1152
HEAD_DIM = 72
PAIR = 144
FF_HERE = 144
TOK = 128
CAP = 64
NZC = 8
NYC = 4
NEX = 8
RY = 64
RZ = 80
EPS = 1e-06
BF = jnp.bfloat16
F32 = jnp.float32
NT = (((1,), (1,)), ((), ()))
MESH = pl.DeviceIdType.MESH


def dot(a, b):
    return jnp.dot(a, b, preferred_element_type=F32)


def dot_nt(a, b):
    return lax.dot_general(a, b, NT, preferred_element_type=F32)


def modulate(values, shift, scale):
    centered = values - jnp.mean(values, axis=-1, keepdims=True)
    spread = jnp.mean(centered * centered, axis=-1, keepdims=True)
    return centered * lax.rsqrt(spread + EPS) * (1.0 + scale) + shift


def gelu(u):
    return 0.5 * u * (1.0 + jnp.tanh(0.7978845608 * (u + 0.044715 * (u * u * u))))


HALO = 0
YP = 2
YZ = 5
ZZ = 19
ZA = 26
ZB = 34
ZC = 42
XX = 50
DI = 58
RE = 65
NSEM = 72


def kernel(
    tok, mod, wqkv, wproj, phase, routes, gates, win, wout, out,
    buf_y, buf_z, buf_x, halo, normed, mask, att, picks, out_buf, in_buf, acc, back, ret,
    send, recv, local,
):
    g = lax.axis_index("gz")
    e = lax.axis_index("ex")
    z, y = g // NYC, g % NYC
    x, core = e // 2, e % 2
    sigma = 1 - 2 * core
    zp = ((z + sigma + NZC) % NZC) * NYC + y
    zm = ((z - sigma + NZC) % NZC) * NYC + y
    y1 = z * NYC + (y + 1) % NYC
    y2 = z * NYC + (y + 2) % NYC
    y3 = z * NYC + (y + 3) % NYC
    gp = (g + 1) % (NZC * NYC)
    gm = (g + NZC * NYC - 1) % (NZC * NYC)
    xp = ((x + 1) % 4) * 2 + core
    xm = ((x + 3) % 4) * 2 + core
    sib = x * 2 + 1 - core

    def remote(src, dst, number, axis, where):
        return pltpu.make_async_remote_copy(
            src_ref=src, dst_ref=dst, send_sem=send.at[number], recv_sem=recv.at[number],
            device_id={axis: where}, device_id_type=MESH,
        )

    def c_halo(k):
        return remote(tok, halo.at[k], HALO + k, "gz", (gp, gm)[k])

    def c_yp(k):
        own = buf_y.at[0, 0, :, 0:RY]
        dst = (buf_y.at[0, 0, :, RY : 2 * RY], buf_y.at[0, 1, :, 0:RY], buf_y.at[0, 1, :, RY : 2 * RY])[k]
        return remote(own, dst, YP + k, "gz", (y1, y3, y2)[k])

    def prior(t):
        return 0 if t <= 2 else t - 2

    def c_yz(t, h):
        return remote(
            buf_y.at[prior(t), h], buf_y.at[t, h], YZ + (t - 1) * 2 + h, "gz", zp if t % 2 else zm
        )

    def c_zz(t):
        return remote(buf_z.at[prior(t), 0], buf_z.at[t, 0], ZZ + t - 1, "gz", zp if t % 2 else zm)

    def c_za(t):
        return remote(buf_z.at[t, 0], buf_z.at[t, 1], ZA + t, "gz", y3 if t % 2 else y1)

    def c_zb(t):
        return remote(buf_z.at[t, 0], buf_z.at[t, 2], ZB + t, "gz", y1 if t % 2 else y3)

    def c_zc(t):
        return remote(buf_z.at[t, 1], buf_z.at[t, 3], ZC + t, "gz", y3 if t % 2 else y1)

    half = 2 * PAIR

    def c_x(k):
        src, dst, where = (
            (buf_x.at[0], buf_x.at[1], sib),
            (buf_x.at[0], buf_x.at[2], xp),
            (buf_x.at[0], buf_x.at[3], xm),
            (buf_x.at[2, 0:half], buf_x.at[6, 0:half], xp),
            (buf_x.at[3, half : 2 * half], buf_x.at[6, half : 2 * half], xm),
            (buf_x.at[2], buf_x.at[4], sib),
            (buf_x.at[3], buf_x.at[5], sib),
            (buf_x.at[6], buf_x.at[7], sib),
        )[k]
        return remote(src, dst, XX + k, "ex", where)

    def c_di(k):
        peer = (e + k) % NEX
        return remote(out_buf.at[peer], in_buf.at[e], DI + k - 1, "ex", peer)

    def c_re(k):
        peer = (e + k) % NEX
        return remote(back.at[peer], ret.at[e], RE + k - 1, "ex", peer)

    def ev_z(t):
        c_zz(t).wait_recv()
        if t <= 5:
            c_zz(t + 2).start()
        c_za(t).start()
        c_zb(t).start()

    def ev_r(t):
        c_za(t).wait_recv()
        c_zc(t).start()

    def ev_y0():
        for k in range(3):
            c_yp(k).wait_recv()
        for h in range(2):
            for t in (1, 2):
                c_yz(t, h).start()

    def ev_y(t, h):
        c_yz(t, h).wait_recv()
        if t <= 5:
            c_yz(t + 2, h).start()

    loads = [
        pltpu.make_async_copy(win.at[0:RY], buf_y.at[0, 0, 0, 0:RY], local.at[0]),
        pltpu.make_async_copy(wout.at[0:RY], buf_y.at[0, 0, 1, 0:RY], local.at[1]),
        pltpu.make_async_copy(win.at[RY:FF_HERE], buf_z.at[0, 0, 0], local.at[2]),
        pltpu.make_async_copy(wout.at[RY:FF_HERE], buf_z.at[0, 0, 1], local.at[3]),
        pltpu.make_async_copy(wproj, buf_x.at[0, 3 * PAIR : 4 * PAIR], local.at[4]),
    ]
    for load in loads:
        load.start()
    barrier = pltpu.get_barrier_semaphore()
    for where in (zp, zm, y1, y2, y3, gp, gm):
        pl.semaphore_signal(barrier, inc=1, device_id={"gz": where}, device_id_type=MESH)
    for k in range(1, NEX):
        pl.semaphore_signal(barrier, inc=1, device_id={"ex": (e + k) % NEX}, device_id_type=MESH)
    eye = (
        lax.broadcasted_iota(jnp.int32, (PAIR, PAIR), 0) == lax.broadcasted_iota(jnp.int32, (PAIR, PAIR), 1)
    ).astype(F32).astype(BF)
    for i in range(3):
        buf_x[0, i * PAIR : (i + 1) * PAIR, :] = dot_nt(eye, wqkv[i]).astype(BF)
    for load in loads:
        load.wait()
    pl.semaphore_wait(barrier, 7 + NEX - 1)

    for k in (2, 0, 1):
        c_yp(k).start()
    for k in range(2):
        c_halo(k).start()
    c_zz(1).start()
    c_zz(2).start()
    c_za(0).start()
    c_zb(0).start()
    for k in (1, 2, 0):
        c_x(k).start()

    normed[0:TOK, :] = modulate(tok[...].astype(F32), mod[0:1, :], mod[1:2, :]).astype(BF)
    phase0, phase1 = phase[2 * e], phase[2 * e + 1]
    rows = lax.broadcasted_iota(jnp.int32, (TOK, 3 * TOK), 0)
    cols = lax.broadcasted_iota(jnp.int32, (TOK, 3 * TOK), 1)
    row_tile = rows >> 6
    col_in = cols & (TOK - 1)
    block = cols >> 7
    offset = jnp.where(block == 2, 1, jnp.where(block == 1, -1, 0))
    shift = jnp.where(row_tile == 0, phase0, phase1)
    here = ((rows & 3) + shift) >> 2
    there = (((col_in & 3) + shift) >> 2) + offset
    plane_block = g + offset
    allowed = (
        (row_tile == (col_in >> 6)) & (here == there) & (plane_block >= 0) & (plane_block < NZC * NYC)
    )
    ones = jnp.where(allowed, 1.0, 0.0).astype(F32)
    mask[0:TOK, :] = ones
    mask[TOK : 2 * TOK, :] = ones
    for k in range(2):
        c_halo(k).wait_recv()
        normed[(k + 1) * TOK : (k + 2) * TOK, :] = modulate(
            halo[k].astype(F32), mod[0:1, :], mod[1:2, :]
        ).astype(BF)
    att[...] = jnp.zeros_like(att)

    def heads(j, carry):
        @pl.when(j == 1)
        def _():
            c_x(0).wait_recv()

        @pl.when(j == 2)
        def _():
            ev_z(1)
            ev_z(2)
            ev_y0()
            ev_z(3)
            ev_z(4)
            ev_r(0)
            ev_z(5)
            ev_z(6)
            c_x(1).wait_recv()
            c_x(3).start()
            c_x(5).start()

        @pl.when(j == 3)
        def _():
            c_x(2).wait_recv()
            c_x(4).start()
            c_x(6).start()
            ev_r(1)
            ev_z(7)

        @pl.when(j == 4)
        def _():
            c_x(5).wait_recv()

        @pl.when(j == 5)
        def _():
            c_x(6).wait_recv()
            ev_r(2)

        @pl.when(j == 6)
        def _():
            ev_y(1, 0)
            ev_y(2, 0)
            c_x(3).wait_recv()
            c_x(4).wait_recv()
            c_x(7).start()

        @pl.when(j == 7)
        def _():
            ev_r(3)
            c_x(7).wait_recv()

        low = lax.broadcasted_iota(jnp.int32, (TOK, PAIR), 1) < HEAD_DIM
        low3 = lax.broadcasted_iota(jnp.int32, (3 * TOK, PAIR), 1) < HEAD_DIM

        def normalise(values, first):
            squares = values * values
            one = jnp.sum(jnp.where(first, squares, 0.0), axis=-1, keepdims=True)
            two = jnp.sum(jnp.where(first, 0.0, squares), axis=-1, keepdims=True)
            return values * jnp.where(
                first,
                lax.rsqrt(one * (1.0 / HEAD_DIM) + EPS),
                lax.rsqrt(two * (1.0 / HEAD_DIM) + EPS),
            )

        query = normalise(dot_nt(normed[0:TOK, :], buf_x[j, 0:PAIR, :]), low)
        keys = normalise(dot_nt(normed[...], buf_x[j, PAIR : 2 * PAIR, :]), low3).astype(BF)
        values = dot_nt(normed[...], buf_x[j, 2 * PAIR : 3 * PAIR, :]).astype(BF)
        both = jnp.concatenate(
            [jnp.where(low, query, 0.0).astype(BF), jnp.where(low, 0.0, query).astype(BF)], axis=0
        )
        raw = jnp.exp(dot_nt(both, keys) * (1.0 / math.sqrt(HEAD_DIM))) * mask[...]
        shares = (raw / jnp.sum(raw, axis=-1, keepdims=True)).astype(BF)
        mixed = dot(shares, values)
        mixture = jnp.where(low, mixed[0:TOK], mixed[TOK : 2 * TOK]).astype(BF)
        att[...] += dot(mixture, buf_x[j, 3 * PAIR : 4 * PAIR, :])
        return carry

    lax.fori_loop(0, NEX, heads, 0)
    ev_y(1, 1)
    ev_y(2, 1)

    residual = tok[...].astype(F32) + mod[2:3, :] * att[...]
    att[...] = residual
    moe_in = modulate(residual, mod[3:4, :], mod[4:5, :]).astype(BF)
    lane = lax.broadcasted_iota(jnp.int32, (TOK, TOK), 1)
    r0, r1 = routes[:, 0:1], routes[:, 1:2]
    member = jnp.where((r0 == lane) | (r1 == lane), 1.0, 0.0).astype(BF)
    earlier = jnp.where(lax.broadcasted_iota(jnp.int32, (TOK, TOK), 0) > lane, 1.0, 0.0).astype(BF)
    spot = dot(earlier, member) + (lane * CAP).astype(F32)
    slots = lax.broadcasted_iota(jnp.int32, (TOK, NEX * CAP), 1).astype(F32)
    chosen = []
    for r in (r0, r1):
        target = jnp.sum(jnp.where(r == lane, spot, 0.0), axis=-1, keepdims=True)
        chosen.append(jnp.where(slots == target, 1.0, 0.0))
    picks[0] = chosen[0].astype(BF)
    picks[1] = chosen[1].astype(BF)
    table = jnp.transpose(chosen[0] + chosen[1]).astype(BF)
    out_buf[...] = dot(table, moe_in).astype(BF).reshape(NEX, CAP, D)
    ev_r(4)
    for k in (4, 5, 3, 2, 6, 1, 7):
        c_di(k).start()
    in_buf[e] = out_buf[e]
    acc[...] = jnp.zeros_like(acc)
    ev_y(3, 0)
    ev_y(4, 0)
    for k in range(1, NEX):
        c_di(k).wait_recv()

    def block_of(t, carry):
        @pl.when(t == 1)
        def _():
            ev_r(5)

        @pl.when(t == 2)
        def _():
            ev_y(3, 1)
            ev_y(4, 1)

        @pl.when(t == 4)
        def _():
            ev_r(6)
            ev_y(5, 0)
            ev_y(6, 0)

        @pl.when(t == 5)
        def _():
            ev_y(5, 1)
            ev_y(6, 1)
            ev_r(7)

        rows_in = in_buf[...].reshape(NEX * CAP, D)

        def part(first, second):
            hidden = gelu(dot_nt(rows_in, first)).astype(BF)
            acc[...] += dot(hidden, second)

        remote(buf_z.at[t, 0], buf_z.at[t, 2], ZB + t, "gz", y1).wait_recv()
        remote(buf_z.at[t, 1], buf_z.at[t, 3], ZC + t, "gz", y1).wait_recv()
        part(
            jnp.concatenate([buf_z[t, i, 0] for i in range(4)], axis=0),
            jnp.concatenate([buf_z[t, i, 1] for i in range(4)], axis=0),
        )

        @pl.when(t == 7)
        def _():
            ev_y(7, 0)
            ev_y(7, 1)

        part(
            jnp.concatenate([buf_y[t, i, 0] for i in range(2)], axis=0),
            jnp.concatenate([buf_y[t, i, 1] for i in range(2)], axis=0),
        )
        return carry

    lax.fori_loop(0, NZC, block_of, 0)

    back[...] = acc[...].astype(BF).reshape(NEX, CAP, D)
    for k in (4, 5, 3, 2, 6, 1, 7):
        c_re(k).start()
    ret[e] = back[e]
    for k in range(1, NEX):
        c_re(k).wait_recv()
    returned = ret[...].reshape(NEX * CAP, D)
    total = gates[:, 0:1] * dot(picks[0], returned) + gates[:, 1:2] * dot(picks[1], returned)
    out[...] = (att[...] + mod[5:6, :] * total).astype(BF)

    for k in range(2):
        c_halo(k).wait_send()
    for k in range(3):
        c_yp(k).wait_send()
    for t in range(1, 8):
        for h in range(2):
            c_yz(t, h).wait_send()
        c_zz(t).wait_send()
    for t in range(8):
        c_za(t).wait_send()
        c_zb(t).wait_send()
        c_zc(t).wait_send()
        c_x(t).wait_send()
    for k in range(1, NEX):
        c_di(k).wait_send()
        c_re(k).wait_send()


def per_device(tokens, modulation, w_qkv, w_proj, phase, routes, gates, w_in, w_out):
    columns, planes, _ = tokens.shape
    vmem = pl.BlockSpec(memory_space=pltpu.VMEM)
    anywhere = pl.BlockSpec(memory_space=pl.ANY)
    updated = pl.pallas_call(
        kernel,
        out_shape=jax.ShapeDtypeStruct((TOK, D), BF),
        in_specs=[
            vmem, vmem, vmem, anywhere, pl.BlockSpec(memory_space=pltpu.SMEM), vmem, vmem, anywhere, anywhere,
        ],
        out_specs=vmem,
        scratch_shapes=[
            pltpu.VMEM((NZC, 2, 2, 2 * RY, D), BF),
            pltpu.VMEM((NZC, NYC, 2, RZ, D), BF),
            pltpu.VMEM((NEX, 4 * PAIR, D), BF),
            pltpu.VMEM((2, TOK, D), BF),
            pltpu.VMEM((3 * TOK, D), BF),
            pltpu.VMEM((2 * TOK, 3 * TOK), F32),
            pltpu.VMEM((TOK, D), F32),
            pltpu.VMEM((2, TOK, NEX * CAP), BF),
            pltpu.VMEM((NEX, CAP, D), BF),
            pltpu.VMEM((NEX, CAP, D), BF),
            pltpu.VMEM((NEX * CAP, D), F32),
            pltpu.VMEM((NEX, CAP, D), BF),
            pltpu.VMEM((NEX, CAP, D), BF),
            pltpu.SemaphoreType.DMA((NSEM,)),
            pltpu.SemaphoreType.DMA((NSEM,)),
            pltpu.SemaphoreType.DMA((5,)),
        ],
        compiler_params=pltpu.CompilerParams(
            collective_id=0, has_side_effects=True, vmem_limit_bytes=60 * 1024 * 1024
        ),
        name="layer",
    )(
        tokens.reshape(TOK, D), modulation, w_qkv, w_proj, phase,
        routes.reshape(TOK, 2), gates.reshape(TOK, 2), w_in[0], w_out[0],
    )
    return updated.reshape(columns, planes, D)


def solution(mesh):
    return jax.shard_map(
        per_device,
        mesh=mesh,
        in_specs=(
            P("ex", "gz", None),
            P(),
            P(None, None, "ex"),
            P("ex", None),
            P(),
            P("ex", "gz", None, None),
            P("ex", "gz", None, None),
            P("ex", "gz", None),
            P("ex", "gz", None),
        ),
        out_specs=P("ex", "gz", None),
        check_vma=False,
    )
```

```python
import functools
import math

import jax
import jax.numpy as jnp
from jax import lax
from jax.experimental import pallas as pl
from jax.experimental.pallas import tpu as pltpu
from jax.sharding import PartitionSpec as P

D = 1152
HEAD_DIM = 72
PAIR = 144
FF_HERE = 144
TOK = 128
CAP = 64
NZC = 8
NYC = 4
NEX = 8
RY = 64
RZ = 80
EPS = 1e-06
BF = jnp.bfloat16
F32 = jnp.float32
NT = (((1,), (1,)), ((), ()))
MESH = pl.DeviceIdType.MESH


def dot(a, b):
    return jnp.dot(a, b, preferred_element_type=F32)


def dot_nt(a, b):
    return lax.dot_general(a, b, NT, preferred_element_type=F32)


def modulate(values, shift, scale):
    centered = values - jnp.mean(values, axis=-1, keepdims=True)
    spread = jnp.mean(centered * centered, axis=-1, keepdims=True)
    return centered * lax.rsqrt(spread + EPS) * (1.0 + scale) + shift


def gelu(u):
    return 0.5 * u * (1.0 + jnp.tanh(0.7978845608 * (u + 0.044715 * (u * u * u))))


HALO = 0
YP = 2
YZ = 5
ZZ = 19
ZA = 26
ZB = 34
ZC = 42
XX = 50
DI = 58
RE = 65
NSEM = 72


def kernel(
    tok, mod, wqkv, wproj, phase, routes, gates, win, wout, out,
    buf_y, buf_z, buf_x, halo, normed, mask, att, picks, out_buf, in_buf, acc, back, ret, weights,
    send, recv, local,
):
    g = lax.axis_index("gz")
    e = lax.axis_index("ex")
    z, y = g // NYC, g % NYC
    x, core = e // 2, e % 2
    sigma = 1 - 2 * core
    zp = ((z + sigma + NZC) % NZC) * NYC + y
    zm = ((z - sigma + NZC) % NZC) * NYC + y
    y1 = z * NYC + (y + 1) % NYC
    y2 = z * NYC + (y + 2) % NYC
    y3 = z * NYC + (y + 3) % NYC
    gp = (g + 1) % (NZC * NYC)
    gm = (g + NZC * NYC - 1) % (NZC * NYC)
    xp = ((x + 1) % 4) * 2 + core
    xm = ((x + 3) % 4) * 2 + core
    sib = x * 2 + 1 - core

    def remote(src, dst, number, axis, where):
        return pltpu.make_async_remote_copy(
            src_ref=src, dst_ref=dst, send_sem=send.at[number], recv_sem=recv.at[number],
            device_id={axis: where}, device_id_type=MESH,
        )

    def c_halo(k):
        return remote(tok, halo.at[k], HALO + k, "gz", (gp, gm)[k])

    def c_yp(k):
        own = buf_y.at[0, 0, :, 0:RY]
        dst = (buf_y.at[0, 0, :, RY : 2 * RY], buf_y.at[0, 1, :, 0:RY], buf_y.at[0, 1, :, RY : 2 * RY])[k]
        return remote(own, dst, YP + k, "gz", (y1, y3, y2)[k])

    def prior(t):
        return 0 if t <= 2 else t - 2

    def c_yz(t, h):
        return remote(
            buf_y.at[prior(t), h], buf_y.at[t, h], YZ + (t - 1) * 2 + h, "gz", zp if t % 2 else zm
        )

    def c_zz(t):
        return remote(buf_z.at[prior(t), 0], buf_z.at[t, 0], ZZ + t - 1, "gz", zp if t % 2 else zm)

    def c_za(t):
        return remote(buf_z.at[t, 0], buf_z.at[t, 1], ZA + t, "gz", y3 if t % 2 else y1)

    def c_zb(t):
        return remote(buf_z.at[t, 0], buf_z.at[t, 2], ZB + t, "gz", y1 if t % 2 else y3)

    def c_zc(t):
        return remote(buf_z.at[t, 1], buf_z.at[t, 3], ZC + t, "gz", y3 if t % 2 else y1)

    half = 2 * PAIR

    def c_x(k):
        src, dst, where = (
            (buf_x.at[0], buf_x.at[1], sib),
            (buf_x.at[0], buf_x.at[2], xp),
            (buf_x.at[0], buf_x.at[3], xm),
            (buf_x.at[2, 0:half], buf_x.at[6, 0:half], xp),
            (buf_x.at[3, half : 2 * half], buf_x.at[6, half : 2 * half], xm),
            (buf_x.at[2], buf_x.at[4], sib),
            (buf_x.at[3], buf_x.at[5], sib),
            (buf_x.at[6], buf_x.at[7], sib),
        )[k]
        return remote(src, dst, XX + k, "ex", where)

    def c_di(k):
        peer = (e + k) % NEX
        return remote(out_buf.at[peer], in_buf.at[e], DI + k - 1, "ex", peer)

    def c_re(k):
        peer = (e + k) % NEX
        return remote(back.at[peer], ret.at[e], RE + k - 1, "ex", peer)

    def ev_z(t):
        c_zz(t).wait_recv()
        if t <= 5:
            c_zz(t + 2).start()
        c_za(t).start()
        c_zb(t).start()

    def ev_r(t):
        c_za(t).wait_recv()
        c_zc(t).start()

    def ev_y0():
        for k in range(3):
            c_yp(k).wait_recv()
        for h in range(2):
            for t in (1, 2):
                c_yz(t, h).start()

    def ev_y(t, h):
        c_yz(t, h).wait_recv()
        if t <= 5:
            c_yz(t + 2, h).start()

    loads = [
        pltpu.make_async_copy(win.at[0:RY], buf_y.at[0, 0, 0, 0:RY], local.at[0]),
        pltpu.make_async_copy(wout.at[0:RY], buf_y.at[0, 0, 1, 0:RY], local.at[1]),
        pltpu.make_async_copy(win.at[RY:FF_HERE], buf_z.at[0, 0, 0], local.at[2]),
        pltpu.make_async_copy(wout.at[RY:FF_HERE], buf_z.at[0, 0, 1], local.at[3]),
        pltpu.make_async_copy(wproj, buf_x.at[0, 3 * PAIR : 4 * PAIR], local.at[4]),
    ] + [
        pltpu.make_async_copy(wqkv.at[i], buf_x.at[0, i * PAIR : (i + 1) * PAIR], local.at[5 + i]) for i in range(3)
    ]
    for load in loads:
        load.start()
    barrier = pltpu.get_barrier_semaphore()
    for where in (zp, zm, y1, y2, y3, gp, gm):
        pl.semaphore_signal(barrier, inc=1, device_id={"gz": where}, device_id_type=MESH)
    for k in range(1, NEX):
        pl.semaphore_signal(barrier, inc=1, device_id={"ex": (e + k) % NEX}, device_id_type=MESH)
    for load in loads:
        load.wait()
    pl.semaphore_wait(barrier, 7 + NEX - 1)

    for k in (2, 0, 1):
        c_yp(k).start()
    for k in range(2):
        c_halo(k).start()
    c_zz(1).start()
    c_zz(2).start()
    c_za(0).start()
    c_zb(0).start()
    for k in (1, 2, 0):
        c_x(k).start()

    normed[0:TOK, :] = modulate(tok[...].astype(F32), mod[0:1, :], mod[1:2, :]).astype(BF)
    phase0, phase1 = phase[2 * e], phase[2 * e + 1]
    rows = lax.broadcasted_iota(jnp.int32, (TOK, 3 * TOK), 0)
    cols = lax.broadcasted_iota(jnp.int32, (TOK, 3 * TOK), 1)
    row_tile = rows >> 6
    col_in = cols & (TOK - 1)
    block = cols >> 7
    offset = jnp.where(block == 2, 1, jnp.where(block == 1, -1, 0))
    shift = jnp.where(row_tile == 0, phase0, phase1)
    here = ((rows & 3) + shift) >> 2
    there = (((col_in & 3) + shift) >> 2) + offset
    plane_block = g + offset
    allowed = (
        (row_tile == (col_in >> 6)) & (here == there) & (plane_block >= 0) & (plane_block < NZC * NYC)
    )
    ones = jnp.where(allowed, 1.0, 0.0).astype(F32)
    mask[0:TOK, :] = ones
    mask[TOK : 2 * TOK, :] = ones
    for k in range(2):
        c_halo(k).wait_recv()
        normed[(k + 1) * TOK : (k + 2) * TOK, :] = modulate(
            halo[k].astype(F32), mod[0:1, :], mod[1:2, :]
        ).astype(BF)
    att[...] = jnp.zeros_like(att)

    def heads(j, carry):
        @pl.when(j == 1)
        def _():
            ev_z(1)
            ev_z(2)
            c_x(0).wait_recv()

        @pl.when(j == 2)
        def _():
            ev_z(3)
            ev_z(4)
            ev_y0()
            ev_r(1)
            ev_r(0)
            ev_z(5)
            ev_z(6)
            c_x(1).wait_recv()
            c_x(3).start()
            c_x(5).start()
            c_x(2).wait_recv()
            c_x(4).start()
            c_x(6).start()

        @pl.when(j == 4)
        def _():
            c_x(5).wait_recv()

        @pl.when(j == 5)
        def _():
            c_x(6).wait_recv()
            ev_r(3)
            ev_y(1, 0)
            ev_y(2, 0)

        @pl.when(j == 6)
        def _():
            ev_r(2)
            c_x(3).wait_recv()
            c_x(4).wait_recv()
            c_x(7).start()

        @pl.when(j == 7)
        def _():
            c_x(7).wait_recv()

        low = lax.broadcasted_iota(jnp.int32, (TOK, PAIR), 1) < HEAD_DIM
        low3 = lax.broadcasted_iota(jnp.int32, (3 * TOK, PAIR), 1) < HEAD_DIM

        def normalise(values, first):
            squares = values * values
            one = jnp.sum(jnp.where(first, squares, 0.0), axis=-1, keepdims=True)
            two = jnp.sum(jnp.where(first, 0.0, squares), axis=-1, keepdims=True)
            return values * jnp.where(
                first,
                lax.rsqrt(one * (1.0 / HEAD_DIM) + EPS),
                lax.rsqrt(two * (1.0 / HEAD_DIM) + EPS),
            )

        query = normalise(dot_nt(normed[0:TOK, :], buf_x[j, 0:PAIR, :]), low)
        keys = normalise(dot_nt(normed[...], buf_x[j, PAIR : 2 * PAIR, :]), low3).astype(BF)
        values = dot_nt(normed[...], buf_x[j, 2 * PAIR : 3 * PAIR, :]).astype(BF)
        both = jnp.concatenate(
            [jnp.where(low, query, 0.0).astype(BF), jnp.where(low, 0.0, query).astype(BF)], axis=0
        )
        raw = jnp.exp(dot_nt(both, keys) * (1.0 / math.sqrt(HEAD_DIM))) * mask[...]
        shares = (raw / jnp.sum(raw, axis=-1, keepdims=True)).astype(BF)
        mixed = dot(shares, values)
        mixture = jnp.where(low, mixed[0:TOK], mixed[TOK : 2 * TOK]).astype(BF)
        att[...] += dot(mixture, buf_x[j, 3 * PAIR : 4 * PAIR, :])
        return carry

    lax.fori_loop(0, NEX, heads, 0)
    ev_y(1, 1)
    ev_y(2, 1)

    residual = tok[...].astype(F32) + mod[2:3, :] * att[...]
    att[...] = residual
    moe_in = modulate(residual, mod[3:4, :], mod[4:5, :]).astype(BF)
    lane = lax.broadcasted_iota(jnp.int32, (TOK, TOK), 1)
    lane_f = lane.astype(F32)
    r0, r1 = (jnp.transpose(jnp.broadcast_to(routes[r : r + 1, :].astype(F32), (TOK, TOK))) for r in range(2))
    gate0, gate1 = (jnp.transpose(jnp.broadcast_to(gates[r : r + 1, :], (TOK, TOK))) for r in range(2))
    weights[...] = jnp.where(lane == 0, gate0, gate1)
    member = jnp.where((r0 == lane_f) | (r1 == lane_f), 1.0, 0.0).astype(BF)
    earlier = jnp.where(lax.broadcasted_iota(jnp.int32, (TOK, TOK), 0) > lane, 1.0, 0.0).astype(BF)
    spot = dot(earlier, member) + (lane * CAP).astype(F32)
    slots = lax.broadcasted_iota(jnp.int32, (TOK, NEX * CAP), 1).astype(F32)
    chosen = []
    for r in (r0, r1):
        target = jnp.sum(jnp.where(r == lane_f, spot, 0.0), axis=-1, keepdims=True)
        chosen.append(jnp.where(slots == target, 1.0, 0.0))
    picks[0] = chosen[0].astype(BF)
    picks[1] = chosen[1].astype(BF)
    table = jnp.transpose(chosen[0] + chosen[1]).astype(BF)
    out_buf[...] = dot(table, moe_in).astype(BF).reshape(NEX, CAP, D)
    for k in (4, 5, 3, 2, 6, 1, 7):
        c_di(k).start()
    ev_r(4)
    in_buf[e] = out_buf[e]
    acc[...] = jnp.zeros_like(acc)
    ev_z(7)
    ev_r(5)
    ev_y(4, 0)
    for k in range(1, NEX):
        c_di(k).wait_recv()

    def block_of(s, carry):
        rows_in = in_buf[...].reshape(NEX * CAP, D)

        def part(first, second):
            hidden = gelu(dot_nt(rows_in, first)).astype(BF)
            acc[...] += dot(hidden, second)

        @pl.when(s == 3)
        def _():
            ev_r(7)
            ev_y(3, 1)

        t = s + 1 - 2 * (s % 2)
        remote(buf_z.at[t, 0], buf_z.at[t, 2], ZB + t, "gz", y1).wait_recv()
        remote(buf_z.at[t, 1], buf_z.at[t, 3], ZC + t, "gz", y1).wait_recv()
        part(
            jnp.concatenate([buf_z[t, i, 0] for i in range(4)], axis=0),
            jnp.concatenate([buf_z[t, i, 1] for i in range(4)], axis=0),
        )

        @pl.when(s == 0)
        def _():
            ev_y(3, 0)

        @pl.when(s == 1)
        def _():
            ev_y(4, 1)

        @pl.when(s == 2)
        def _():
            ev_r(6)

        @pl.when(s == 3)
        def _():
            ev_y(6, 0)

        @pl.when(s == 4)
        def _():
            ev_y(5, 0)

        @pl.when(s == 5)
        def _():
            ev_y(6, 1)
            ev_y(5, 1)

        @pl.when(s == 7)
        def _():
            ev_y(7, 0)
            ev_y(7, 1)

        part(
            jnp.concatenate([buf_y[s, i, 0] for i in range(2)], axis=0),
            jnp.concatenate([buf_y[s, i, 1] for i in range(2)], axis=0),
        )
        return carry

    lax.fori_loop(0, NZC, block_of, 0)

    back[...] = acc[...].astype(BF).reshape(NEX, CAP, D)
    for k in (4, 5, 3, 2, 6, 1, 7):
        c_re(k).start()
    ret[e] = back[e]
    for k in range(1, NEX):
        c_re(k).wait_recv()
    returned = ret[...].reshape(NEX * CAP, D)
    total = weights[:, 0:1] * dot(picks[0], returned) + weights[:, 1:2] * dot(picks[1], returned)
    out[...] = (att[...] + mod[5:6, :] * total).astype(BF)

    for k in range(2):
        c_halo(k).wait_send()
    for k in range(3):
        c_yp(k).wait_send()
    for t in range(1, 8):
        for h in range(2):
            c_yz(t, h).wait_send()
        c_zz(t).wait_send()
    for t in range(8):
        c_za(t).wait_send()
        c_zb(t).wait_send()
        c_zc(t).wait_send()
        c_x(t).wait_send()
    for k in range(1, NEX):
        c_di(k).wait_send()
        c_re(k).wait_send()


def per_device(tokens, modulation, w_qkv, w_proj, phase, routes, gates, w_in, w_out):
    columns, planes, _ = tokens.shape
    vmem = pl.BlockSpec(memory_space=pltpu.VMEM)
    anywhere = pl.BlockSpec(memory_space=pl.ANY)
    updated = pl.pallas_call(
        kernel,
        out_shape=jax.ShapeDtypeStruct((TOK, D), BF),
        in_specs=[
            vmem, vmem, anywhere, anywhere, pl.BlockSpec(memory_space=pltpu.SMEM), vmem, vmem, anywhere, anywhere,
        ],
        out_specs=vmem,
        scratch_shapes=[
            pltpu.VMEM((NZC, 2, 2, 2 * RY, D), BF),
            pltpu.VMEM((NZC, NYC, 2, RZ, D), BF),
            pltpu.VMEM((NEX, 4 * PAIR, D), BF),
            pltpu.VMEM((2, TOK, D), BF),
            pltpu.VMEM((3 * TOK, D), BF),
            pltpu.VMEM((2 * TOK, 3 * TOK), F32),
            pltpu.VMEM((TOK, D), F32),
            pltpu.VMEM((2, TOK, NEX * CAP), BF),
            pltpu.VMEM((NEX, CAP, D), BF),
            pltpu.VMEM((NEX, CAP, D), BF),
            pltpu.VMEM((NEX * CAP, D), F32),
            pltpu.VMEM((NEX, CAP, D), BF),
            pltpu.VMEM((NEX, CAP, D), BF),
            pltpu.VMEM((TOK, TOK), F32),
            pltpu.SemaphoreType.DMA((NSEM,)),
            pltpu.SemaphoreType.DMA((NSEM,)),
            pltpu.SemaphoreType.DMA((8,)),
        ],
        compiler_params=pltpu.CompilerParams(
            collective_id=0, has_side_effects=True, vmem_limit_bytes=60 * 1024 * 1024
        ),
        name="layer",
    )(
        tokens.reshape(TOK, D), modulation, jnp.swapaxes(w_qkv, 1, 2), w_proj, phase,
        routes.reshape(TOK, 2).T, gates.reshape(TOK, 2).T, w_in[0], w_out[0],
    )
    return updated.reshape(columns, planes, D)


def solution(mesh):
    return jax.shard_map(
        per_device,
        mesh=mesh,
        in_specs=(
            P("ex", "gz", None),
            P(),
            P(None, None, "ex"),
            P("ex", None),
            P(),
            P("ex", "gz", None, None),
            P("ex", "gz", None, None),
            P("ex", "gz", None),
            P("ex", "gz", None),
        ),
        out_specs=P("ex", "gz", None),
        check_vma=False,
    )
```

```python
import functools
import math

import jax
import jax.numpy as jnp
from jax import lax
from jax.experimental import pallas as pl
from jax.experimental.pallas import tpu as pltpu
from jax.sharding import PartitionSpec as P

D = 1152
HEAD_DIM = 72
PAIR = 144
FF_HERE = 144
TOK = 128
CAP = 64
NZC = 8
NYC = 4
NEX = 8
RY = 64
RZ = 80
EPS = 1e-06
BF = jnp.bfloat16
F32 = jnp.float32
NT = (((1,), (1,)), ((), ()))
MESH = pl.DeviceIdType.MESH


def dot(a, b):
    return jnp.dot(a, b, preferred_element_type=F32)


def dot_nt(a, b):
    return lax.dot_general(a, b, NT, preferred_element_type=F32)


def modulate(values, shift, scale):
    centered = values - jnp.mean(values, axis=-1, keepdims=True)
    spread = jnp.mean(centered * centered, axis=-1, keepdims=True)
    return centered * lax.rsqrt(spread + EPS) * (1.0 + scale) + shift


def gelu(u):
    return 0.5 * u * (1.0 + jnp.tanh(0.7978845608 * (u + 0.044715 * (u * u * u))))


HALO = 0
YP = 2
YZ = 5
ZZ = 19
ZA = 26
ZB = 34
ZC = 42
XX = 50
DI = 58
RE = 65
NSEM = 72


def kernel(
    tok, mod, wqkv, wproj, phase, routes, gates, win, wout, out,
    buf_y, buf_z, buf_x, halo, normed, mask, att, picks, out_buf, in_buf, acc, back, ret, weights,
    send, recv, local,
):
    g = lax.axis_index("gz")
    e = lax.axis_index("ex")
    z, y = g // NYC, g % NYC
    x, core = e // 2, e % 2
    sigma = 1 - 2 * core
    zp = ((z + sigma + NZC) % NZC) * NYC + y
    zm = ((z - sigma + NZC) % NZC) * NYC + y
    y1 = z * NYC + (y + 1) % NYC
    y2 = z * NYC + (y + 2) % NYC
    y3 = z * NYC + (y + 3) % NYC
    gp = (g + 1) % (NZC * NYC)
    gm = (g + NZC * NYC - 1) % (NZC * NYC)
    xp = ((x + 1) % 4) * 2 + core
    xm = ((x + 3) % 4) * 2 + core
    sib = x * 2 + 1 - core

    def remote(src, dst, number, axis, where):
        return pltpu.make_async_remote_copy(
            src_ref=src, dst_ref=dst, send_sem=send.at[number], recv_sem=recv.at[number],
            device_id={axis: where}, device_id_type=MESH,
        )

    def c_halo(k):
        return remote(tok, halo.at[k], HALO + k, "gz", (gp, gm)[k])

    def c_yp(k):
        own = buf_y.at[0, 0, :, 0:RY]
        dst = (buf_y.at[0, 0, :, RY : 2 * RY], buf_y.at[0, 1, :, 0:RY], buf_y.at[0, 1, :, RY : 2 * RY])[k]
        return remote(own, dst, YP + k, "gz", (y1, y3, y2)[k])

    def prior(t):
        return 0 if t <= 2 else t - 2

    def c_yz(t, h):
        return remote(
            buf_y.at[prior(t), h], buf_y.at[t, h], YZ + (t - 1) * 2 + h, "gz", zp if t % 2 else zm
        )

    def c_zz(t):
        return remote(buf_z.at[prior(t), 0], buf_z.at[t, 0], ZZ + t - 1, "gz", zp if t % 2 else zm)

    def c_za(t):
        return remote(buf_z.at[t, 0], buf_z.at[t, 1], ZA + t, "gz", y3 if t % 2 else y1)

    def c_zb(t):
        return remote(buf_z.at[t, 0], buf_z.at[t, 2], ZB + t, "gz", y1 if t % 2 else y3)

    def c_zc(t):
        return remote(buf_z.at[t, 1], buf_z.at[t, 3], ZC + t, "gz", y3 if t % 2 else y1)

    half = 2 * PAIR

    def c_x(k):
        src, dst, where = (
            (buf_x.at[0], buf_x.at[1], sib),
            (buf_x.at[0], buf_x.at[2], xp),
            (buf_x.at[0], buf_x.at[3], xm),
            (buf_x.at[2, 0:half], buf_x.at[6, 0:half], xp),
            (buf_x.at[3, half : 2 * half], buf_x.at[6, half : 2 * half], xm),
            (buf_x.at[2], buf_x.at[4], sib),
            (buf_x.at[3], buf_x.at[5], sib),
            (buf_x.at[6], buf_x.at[7], sib),
        )[k]
        return remote(src, dst, XX + k, "ex", where)

    def c_di(k):
        peer = (e + k) % NEX
        return remote(out_buf.at[peer], in_buf.at[e], DI + k - 1, "ex", peer)

    def c_re(k):
        peer = (e + k) % NEX
        return remote(back.at[peer], ret.at[e], RE + k - 1, "ex", peer)

    def ev_z(t):
        c_zz(t).wait_recv()
        if t <= 5:
            c_zz(t + 2).start()
        c_za(t).start()
        c_zb(t).start()

    def ev_r(t):
        c_za(t).wait_recv()
        c_zc(t).start()

    def ev_y0():
        for k in range(3):
            c_yp(k).wait_recv()
        for h in range(2):
            for t in (1, 2):
                c_yz(t, h).start()

    def ev_y(t, h):
        c_yz(t, h).wait_recv()
        if t <= 5:
            c_yz(t + 2, h).start()

    loads = [
        pltpu.make_async_copy(win.at[0:RY], buf_y.at[0, 0, 0, 0:RY], local.at[0]),
        pltpu.make_async_copy(wout.at[0:RY], buf_y.at[0, 0, 1, 0:RY], local.at[1]),
        pltpu.make_async_copy(win.at[RY:FF_HERE], buf_z.at[0, 0, 0], local.at[2]),
        pltpu.make_async_copy(wout.at[RY:FF_HERE], buf_z.at[0, 0, 1], local.at[3]),
        pltpu.make_async_copy(wproj, buf_x.at[0, 3 * PAIR : 4 * PAIR], local.at[4]),
    ] + [
        pltpu.make_async_copy(wqkv.at[i], buf_x.at[0, i * PAIR : (i + 1) * PAIR], local.at[5 + i]) for i in range(3)
    ]
    for load in loads:
        load.start()
    barrier = pltpu.get_barrier_semaphore()
    for where in (zp, zm, y1, y2, y3, gp, gm):
        pl.semaphore_signal(barrier, inc=1, device_id={"gz": where}, device_id_type=MESH)
    for k in range(1, NEX):
        pl.semaphore_signal(barrier, inc=1, device_id={"ex": (e + k) % NEX}, device_id_type=MESH)
    for load in loads[0:4]:
        load.wait()
    pl.semaphore_wait(barrier, 7 + NEX - 1)

    c_zz(1).start()
    c_zz(2).start()
    for k in (2, 0, 1):
        c_yp(k).start()
    c_za(0).start()
    c_zb(0).start()
    for k in range(2):
        c_halo(k).start()
    for load in loads[4:8]:
        load.wait()
    for k in (1, 2, 0):
        c_x(k).start()

    normed[0:TOK, :] = modulate(tok[...].astype(F32), mod[0:1, :], mod[1:2, :]).astype(BF)
    phase0, phase1 = phase[2 * e], phase[2 * e + 1]
    rows = lax.broadcasted_iota(jnp.int32, (TOK, 3 * TOK), 0)
    cols = lax.broadcasted_iota(jnp.int32, (TOK, 3 * TOK), 1)
    row_tile = rows >> 6
    col_in = cols & (TOK - 1)
    block = cols >> 7
    offset = jnp.where(block == 2, 1, jnp.where(block == 1, -1, 0))
    shift = jnp.where(row_tile == 0, phase0, phase1)
    here = ((rows & 3) + shift) >> 2
    there = (((col_in & 3) + shift) >> 2) + offset
    plane_block = g + offset
    allowed = (
        (row_tile == (col_in >> 6)) & (here == there) & (plane_block >= 0) & (plane_block < NZC * NYC)
    )
    ones = jnp.where(allowed, 1.0, 0.0).astype(F32)
    mask[0:TOK, :] = ones
    mask[TOK : 2 * TOK, :] = ones
    for k in range(2):
        c_halo(k).wait_recv()
        normed[(k + 1) * TOK : (k + 2) * TOK, :] = modulate(
            halo[k].astype(F32), mod[0:1, :], mod[1:2, :]
        ).astype(BF)
    att[...] = jnp.zeros_like(att)
    ev_z(1)
    ev_z(2)

    def heads(j, carry):
        @pl.when(j == 1)
        def _():
            c_x(0).wait_recv()

        @pl.when(j == 2)
        def _():
            ev_z(3)
            ev_z(4)
            ev_y0()
            ev_r(1)
            ev_r(0)
            ev_z(5)
            ev_z(6)
            c_x(1).wait_recv()
            c_x(3).start()
            c_x(5).start()
            c_x(2).wait_recv()
            c_x(4).start()
            c_x(6).start()

        @pl.when(j == 4)
        def _():
            c_x(5).wait_recv()

        @pl.when(j == 5)
        def _():
            c_x(6).wait_recv()
            ev_r(3)
            ev_y(1, 0)
            ev_y(2, 0)

        @pl.when(j == 6)
        def _():
            ev_r(2)
            c_x(3).wait_recv()
            c_x(4).wait_recv()
            c_x(7).start()

        @pl.when(j == 7)
        def _():
            c_x(7).wait_recv()

        low = lax.broadcasted_iota(jnp.int32, (TOK, PAIR), 1) < HEAD_DIM
        low3 = lax.broadcasted_iota(jnp.int32, (3 * TOK, PAIR), 1) < HEAD_DIM

        def normalise(values, first):
            squares = values * values
            one = jnp.sum(jnp.where(first, squares, 0.0), axis=-1, keepdims=True)
            two = jnp.sum(jnp.where(first, 0.0, squares), axis=-1, keepdims=True)
            return values * jnp.where(
                first,
                lax.rsqrt(one * (1.0 / HEAD_DIM) + EPS),
                lax.rsqrt(two * (1.0 / HEAD_DIM) + EPS),
            )

        query = normalise(dot_nt(normed[0:TOK, :], buf_x[j, 0:PAIR, :]), low)
        keys = normalise(dot_nt(normed[...], buf_x[j, PAIR : 2 * PAIR, :]), low3).astype(BF)
        values = dot_nt(normed[...], buf_x[j, 2 * PAIR : 3 * PAIR, :]).astype(BF)
        both = jnp.concatenate(
            [jnp.where(low, query, 0.0).astype(BF), jnp.where(low, 0.0, query).astype(BF)], axis=0
        )
        raw = jnp.exp(dot_nt(both, keys) * (1.0 / math.sqrt(HEAD_DIM))) * mask[...]
        shares = (raw / jnp.sum(raw, axis=-1, keepdims=True)).astype(BF)
        mixed = dot(shares, values)
        mixture = jnp.where(low, mixed[0:TOK], mixed[TOK : 2 * TOK]).astype(BF)
        att[...] += dot(mixture, buf_x[j, 3 * PAIR : 4 * PAIR, :])
        return carry

    lax.fori_loop(0, NEX, heads, 0)
    ev_y(1, 1)
    ev_y(2, 1)

    residual = tok[...].astype(F32) + mod[2:3, :] * att[...]
    att[...] = residual
    moe_in = modulate(residual, mod[3:4, :], mod[4:5, :]).astype(BF)
    lane = lax.broadcasted_iota(jnp.int32, (TOK, TOK), 1)
    lane_f = lane.astype(F32)
    r0, r1 = (jnp.transpose(jnp.broadcast_to(routes[r : r + 1, :].astype(F32), (TOK, TOK))) for r in range(2))
    gate0, gate1 = (jnp.transpose(jnp.broadcast_to(gates[r : r + 1, :], (TOK, TOK))) for r in range(2))
    weights[...] = jnp.where(lane == 0, gate0, gate1)
    member = jnp.where((r0 == lane_f) | (r1 == lane_f), 1.0, 0.0).astype(BF)
    earlier = jnp.where(lax.broadcasted_iota(jnp.int32, (TOK, TOK), 0) > lane, 1.0, 0.0).astype(BF)
    spot = dot(earlier, member) + (lane * CAP).astype(F32)
    slots = lax.broadcasted_iota(jnp.int32, (TOK, NEX * CAP), 1).astype(F32)
    chosen = []
    for r in (r0, r1):
        target = jnp.sum(jnp.where(r == lane_f, spot, 0.0), axis=-1, keepdims=True)
        chosen.append(jnp.where(slots == target, 1.0, 0.0))
    picks[0] = chosen[0].astype(BF)
    picks[1] = chosen[1].astype(BF)
    table = jnp.transpose(chosen[0] + chosen[1]).astype(BF)
    out_buf[...] = dot(table, moe_in).astype(BF).reshape(NEX, CAP, D)
    for k in (4, 5, 3, 2, 6, 1, 7):
        c_di(k).start()
    ev_r(4)
    in_buf[e] = out_buf[e]
    acc[...] = jnp.zeros_like(acc)
    ev_z(7)
    ev_r(5)
    ev_y(4, 0)
    for k in range(1, NEX):
        c_di(k).wait_recv()

    def block_of(s, carry):
        rows_in = in_buf[...].reshape(NEX * CAP, D)

        def part(first, second):
            hidden = gelu(dot_nt(rows_in, first)).astype(BF)
            acc[...] += dot(hidden, second)

        @pl.when(s == 3)
        def _():
            ev_r(7)
            ev_y(3, 1)

        t = s + 1 - 2 * (s % 2)
        remote(buf_z.at[t, 0], buf_z.at[t, 2], ZB + t, "gz", y1).wait_recv()
        remote(buf_z.at[t, 1], buf_z.at[t, 3], ZC + t, "gz", y1).wait_recv()
        part(
            jnp.concatenate([buf_z[t, i, 0] for i in range(4)], axis=0),
            jnp.concatenate([buf_z[t, i, 1] for i in range(4)], axis=0),
        )

        @pl.when(s == 0)
        def _():
            ev_y(3, 0)

        @pl.when(s == 1)
        def _():
            ev_y(4, 1)

        @pl.when(s == 2)
        def _():
            ev_r(6)

        @pl.when(s == 3)
        def _():
            ev_y(6, 0)

        @pl.when(s == 4)
        def _():
            ev_y(5, 0)

        @pl.when(s == 5)
        def _():
            ev_y(6, 1)
            ev_y(5, 1)

        @pl.when(s == 7)
        def _():
            ev_y(7, 0)
            ev_y(7, 1)

        part(
            jnp.concatenate([buf_y[s, i, 0] for i in range(2)], axis=0),
            jnp.concatenate([buf_y[s, i, 1] for i in range(2)], axis=0),
        )
        return carry

    lax.fori_loop(0, NZC, block_of, 0)

    back[...] = acc[...].astype(BF).reshape(NEX, CAP, D)
    for k in (4, 5, 3, 2, 6, 1, 7):
        c_re(k).start()
    ret[e] = back[e]
    for k in range(1, NEX):
        c_re(k).wait_recv()
    returned = ret[...].reshape(NEX * CAP, D)
    total = weights[:, 0:1] * dot(picks[0], returned) + weights[:, 1:2] * dot(picks[1], returned)
    out[...] = (att[...] + mod[5:6, :] * total).astype(BF)

    for k in range(2):
        c_halo(k).wait_send()
    for k in range(3):
        c_yp(k).wait_send()
    for t in range(1, 8):
        for h in range(2):
            c_yz(t, h).wait_send()
        c_zz(t).wait_send()
    for t in range(8):
        c_za(t).wait_send()
        c_zb(t).wait_send()
        c_zc(t).wait_send()
        c_x(t).wait_send()
    for k in range(1, NEX):
        c_di(k).wait_send()
        c_re(k).wait_send()


def per_device(tokens, modulation, w_qkv, w_proj, phase, routes, gates, w_in, w_out):
    columns, planes, _ = tokens.shape
    vmem = pl.BlockSpec(memory_space=pltpu.VMEM)
    anywhere = pl.BlockSpec(memory_space=pl.ANY)
    updated = pl.pallas_call(
        kernel,
        out_shape=jax.ShapeDtypeStruct((TOK, D), BF),
        in_specs=[
            vmem, vmem, anywhere, anywhere, pl.BlockSpec(memory_space=pltpu.SMEM), vmem, vmem, anywhere, anywhere,
        ],
        out_specs=vmem,
        scratch_shapes=[
            pltpu.VMEM((NZC, 2, 2, 2 * RY, D), BF),
            pltpu.VMEM((NZC, NYC, 2, RZ, D), BF),
            pltpu.VMEM((NEX, 4 * PAIR, D), BF),
            pltpu.VMEM((2, TOK, D), BF),
            pltpu.VMEM((3 * TOK, D), BF),
            pltpu.VMEM((2 * TOK, 3 * TOK), F32),
            pltpu.VMEM((TOK, D), F32),
            pltpu.VMEM((2, TOK, NEX * CAP), BF),
            pltpu.VMEM((NEX, CAP, D), BF),
            pltpu.VMEM((NEX, CAP, D), BF),
            pltpu.VMEM((NEX * CAP, D), F32),
            pltpu.VMEM((NEX, CAP, D), BF),
            pltpu.VMEM((NEX, CAP, D), BF),
            pltpu.VMEM((TOK, TOK), F32),
            pltpu.SemaphoreType.DMA((NSEM,)),
            pltpu.SemaphoreType.DMA((NSEM,)),
            pltpu.SemaphoreType.DMA((8,)),
        ],
        compiler_params=pltpu.CompilerParams(
            collective_id=0, has_side_effects=True, vmem_limit_bytes=60 * 1024 * 1024
        ),
        name="layer",
    )(
        tokens.reshape(TOK, D), modulation, jnp.swapaxes(w_qkv, 1, 2), w_proj, phase,
        routes.reshape(TOK, 2).T, gates.reshape(TOK, 2).T, w_in[0], w_out[0],
    )
    return updated.reshape(columns, planes, D)


def solution(mesh):
    return jax.shard_map(
        per_device,
        mesh=mesh,
        in_specs=(
            P("ex", "gz", None),
            P(),
            P(None, None, "ex"),
            P("ex", None),
            P(),
            P("ex", "gz", None, None),
            P("ex", "gz", None, None),
            P("ex", "gz", None),
            P("ex", "gz", None),
        ),
        out_specs=P("ex", "gz", None),
        check_vma=False,
    )
```
